768 devices in a mesh: rows: 96 (over z, y), heads: 8 (over x, core).
Axes of the slice: x: 4, y: 8, z: 12, core: 2. Of those that a mesh axis runs over, the one named last changes fastest.
Arguments:
- queries: bfloat16 [49152, 1024], P('rows', 'heads'), may hold values from -6 to 6
- key_vectors: bfloat16 [49152, 1024], P('rows', 'heads'), may hold values from -6 to 6
- value_vectors: bfloat16 [49152, 1024], P('rows', 'heads'), may hold values from -120 to 120
- gating: bfloat16 [49152, 1024], P('rows', 'heads'), may hold values from -6 to 6
- bounds: int32 [2, 49152], P(None, 'rows'), may hold values from 0 to 49151, as said below
- cotangent: bfloat16 [49152, 1024], P('rows', 'heads'), may hold values from -6 to 6
Outputs:
- layer_out: bfloat16 [49152, 1024], P('rows', 'heads')
- grad_queries: bfloat16 [49152, 1024], P('rows', 'heads')
- grad_keys: bfloat16 [49152, 1024], P('rows', 'heads')
- grad_values: bfloat16 [49152, 1024], P('rows', 'heads')
- grad_gating: bfloat16 [49152, 1024], P('rows', 'heads')
The draws below stay inside these ranges and needn't reach their ends.
Inputs may be any that keep to these rules, and one draw needn't show every extreme that they name: bounds[0, r] and bounds[1, r] are the first and the last row of the history that holds row r; histories are runs of consecutive rows that cover all 49152 rows, each at most 1024 rows long, and one of them exactly that long.
All inputs are finite; a program needn't handle non-finite values.
Results may differ from the reference program's by a relative error of at most 0.006.
Values may be sent and summed in bfloat16 or wider, within the bound.
A program may use at most 32 MiB of HBM per device.

```python
import math
import jax
import jax.numpy as jnp
from jax import lax

DH = 128
ROWS_DEV = 512
REACH = 2
HEADS = 8
TOTAL = 49152


def draw_bounds(key, part):
    longest = REACH * ROWS_DEV
    cut_row = TOTAL - longest - 1
    first_key, second_key = jax.random.split(jax.random.fold_in(key, 7), 2)
    halvings = jax.random.randint(first_key, (TOTAL,), 0, 6)
    nominal = jnp.right_shift(jnp.full((TOTAL,), longest, jnp.int32), halvings.astype(jnp.int32))
    trimmed = jax.random.randint(second_key, (TOTAL,), 0, 1 << 20) % jnp.maximum(nominal // 2, 1)
    lengths = jnp.maximum(nominal - trimmed, 1).astype(jnp.int32)
    user_ends = jnp.cumsum(lengths).astype(jnp.int32)
    user_starts = user_ends - lengths
    indices_all = jnp.arange(TOTAL, dtype=jnp.int32)
    owners = jnp.searchsorted(user_ends, indices_all, side='right').astype(jnp.int32)
    head_first = user_starts[owners]
    head_last = jnp.minimum(user_ends[owners] - 1, cut_row - 1)
    tail_first = jnp.where(indices_all == TOTAL - 1, TOTAL - 1, cut_row).astype(jnp.int32)
    tail_last = jnp.where(indices_all == TOTAL - 1, TOTAL - 1, TOTAL - 2).astype(jnp.int32)
    in_head = indices_all < cut_row
    first_rows = jnp.where(in_head, head_first, tail_first)
    last_rows = jnp.where(in_head, head_last, tail_last)
    return jnp.stack([first_rows, last_rows]).astype(jnp.int32)


def draw_value_vectors(key, part):
    columns_all = HEADS * DH
    first_key, second_key, third_key = jax.random.split(jax.random.fold_in(key, 11), 3)
    head_ids = jnp.arange(columns_all, dtype=jnp.int32) // DH
    rising = 3.0 ** (head_ids.astype(jnp.float32) / max(HEADS - 1, 1))
    column_scale = jnp.exp(jax.random.uniform(first_key, (columns_all,), jnp.float32, 0.0, math.log(10.0)))
    row_scale = jnp.exp(jax.random.uniform(second_key, (TOTAL, 1), jnp.float32, 0.0, math.log(10.0)))
    spread = rising[None, :] * column_scale[None, :] * row_scale / 10.0
    entries = jnp.clip(jax.random.normal(third_key, (TOTAL, columns_all), jnp.float32), -4.0, 4.0)
    return (entries * spread).astype(jnp.bfloat16)


def steps_of(key, extent, cuts, low, largest):
    def one(position, parts):
        heights = jax.random.uniform(jax.random.fold_in(jax.random.fold_in(key, 6), position), (parts,), jnp.float32, low / len(cuts), largest / len(cuts))
        return jnp.repeat(jnp.exp(heights), extent[position] // parts).reshape((-1,) + (1,) * (len(extent) - position - 1))

    level = one(*cuts[0])
    for cut in cuts[1:]:
        level = level * one(*cut)
    return level


def centred(key, extent, scale, bound, shards=(), kind=jnp.bfloat16):
    loudness = steps_of(key, extent, shards, -0.22, 0.18) if shards else 1.0
    values = jax.random.normal(key, extent, jnp.float32) * scale * loudness
    return jnp.minimum(jnp.maximum(values, -bound), bound).astype(kind)


def setup_inputs(seed: int = 0) -> dict:
    arg_keys = jax.random.split(jax.random.key(seed), 7)
    return {
        "queries": centred(arg_keys[0], (TOTAL, HEADS * DH), 1.0, 6.0, ((0, 96), (1, 8))),
        "key_vectors": centred(arg_keys[1], (TOTAL, HEADS * DH), 1.0, 6.0, ((0, 96), (1, 8))),
        "value_vectors": draw_value_vectors(jax.random.fold_in(arg_keys[6], 71), 0),
        "gating": centred(arg_keys[3], (TOTAL, HEADS * DH), 1.0, 6.0, ((0, 96), (1, 8))),
        "bounds": draw_bounds(jax.random.fold_in(arg_keys[6], 71), 0),
        "cotangent": centred(arg_keys[5], (TOTAL, HEADS * DH), 1.0, 6.0, ((0, 96), (1, 8))),
    }


EPSILON = 1e-05

def silu_parts(query_tile, key_tile, allowed, factor):
    scores = jnp.einsum('qhd,khd->hqk', query_tile.astype(jnp.float32), key_tile.astype(jnp.float32)) * factor
    sigmoid = jax.nn.sigmoid(scores)
    weights = jnp.where(allowed[None], scores * sigmoid, 0.0).astype(jnp.bfloat16)
    return (scores, sigmoid, weights)

def reference(queries, key_vectors, value_vectors, gating, bounds, cotangent):
    factor = DH ** (-0.5)
    margin = REACH * ROWS_DEV
    window_size = (REACH + 1) * ROWS_DEV
    block_count = TOTAL // ROWS_DEV
    features = HEADS * DH
    query_all = queries.reshape(TOTAL, HEADS, DH)
    key_pad = jnp.concatenate([jnp.zeros((margin, HEADS, DH), key_vectors.dtype), key_vectors.reshape(TOTAL, HEADS, DH)], 0)
    value_pad = jnp.concatenate([jnp.zeros((margin, HEADS, DH), value_vectors.dtype), value_vectors.reshape(TOTAL, HEADS, DH)], 0)
    first_rows = bounds[0]
    local_rows = jnp.arange(ROWS_DEV, dtype=jnp.int32)
    window_rows = jnp.arange(window_size, dtype=jnp.int32)

    def tile_inputs(tile_index):
        begin_row = tile_index * ROWS_DEV
        query_tile = lax.dynamic_slice_in_dim(query_all, begin_row, ROWS_DEV, 0)
        key_tile = lax.dynamic_slice_in_dim(key_pad, begin_row, window_size, 0)
        value_tile = lax.dynamic_slice_in_dim(value_pad, begin_row, window_size, 0)
        starts = lax.dynamic_slice_in_dim(first_rows, begin_row, ROWS_DEV, 0)
        row_ids = begin_row + local_rows
        key_ids = begin_row - margin + window_rows
        allowed = (key_ids[None, :] >= starts[:, None]) & (key_ids[None, :] <= row_ids[:, None])
        return (query_tile, key_tile, value_tile, allowed)

    def forward_block(tile_index):
        query_tile, key_tile, value_tile, allowed = tile_inputs(tile_index)
        weights = silu_parts(query_tile, key_tile, allowed, factor)[2]
        return jnp.einsum('hqk,khd->qhd', weights.astype(jnp.float32), value_tile.astype(jnp.float32))
    tile_indices = jnp.arange(block_count, dtype=jnp.int32)
    attended = lax.map(forward_block, tile_indices).reshape(TOTAL, features)
    total_sum = lax.optimization_barrier(jnp.sum(attended, axis=1, keepdims=True))
    square_sum = lax.optimization_barrier(jnp.sum(attended * attended, axis=1, keepdims=True))
    average = total_sum / features
    variance = square_sum / features - average * average
    inverse = lax.rsqrt(variance + EPSILON)
    normed = (attended - average) * inverse
    gate_float = gating.astype(jnp.float32)
    layer_out = (normed * gate_float).astype(jnp.bfloat16)
    upstream = cotangent.astype(jnp.float32)
    grad_gating = (upstream * normed).astype(jnp.bfloat16)
    scaled = upstream * gate_float
    grad_sum = lax.optimization_barrier(jnp.sum(scaled, axis=1, keepdims=True))
    cross_sum = lax.optimization_barrier(jnp.sum(scaled * normed, axis=1, keepdims=True))
    delta_rows = (inverse * (scaled - grad_sum / features - normed * (cross_sum / features))).astype(jnp.bfloat16)
    delta_all = delta_rows.reshape(TOTAL, HEADS, DH)

    def backward_block(accumulated, tile_index):
        grad_key_pad, grad_value_pad = accumulated
        query_tile, key_tile, value_tile, allowed = tile_inputs(tile_index)
        scores, sigmoid, weights = silu_parts(query_tile, key_tile, allowed, factor)
        begin_row = tile_index * ROWS_DEV
        delta_tile = lax.dynamic_slice_in_dim(delta_all, begin_row, ROWS_DEV, 0)
        pulled = jnp.einsum('qhd,khd->hqk', delta_tile.astype(jnp.float32), value_tile.astype(jnp.float32))
        score_grad = jnp.where(allowed[None], pulled * sigmoid * (1.0 + scores * (1.0 - sigmoid)), 0.0).astype(jnp.bfloat16)
        grad_query = (jnp.einsum('hqk,khd->qhd', score_grad.astype(jnp.float32), key_tile.astype(jnp.float32)) * factor).astype(jnp.bfloat16)
        key_add = jnp.einsum('hqk,qhd->khd', score_grad.astype(jnp.float32), query_tile.astype(jnp.float32)) * factor
        value_add = jnp.einsum('hqk,qhd->khd', weights.astype(jnp.float32), delta_tile.astype(jnp.float32))
        grad_key_pad = lax.dynamic_update_slice_in_dim(grad_key_pad, lax.dynamic_slice_in_dim(grad_key_pad, begin_row, window_size, 0) + key_add, begin_row, 0)
        grad_value_pad = lax.dynamic_update_slice_in_dim(grad_value_pad, lax.dynamic_slice_in_dim(grad_value_pad, begin_row, window_size, 0) + value_add, begin_row, 0)
        return ((grad_key_pad, grad_value_pad), grad_query)
    empty_pad = jnp.zeros((TOTAL + margin, HEADS, DH), jnp.float32)
    sums_final, grad_blocks = lax.scan(backward_block, (empty_pad, empty_pad), tile_indices)
    grad_queries = grad_blocks.reshape(TOTAL, features)
    grad_keys = sums_final[0][margin:].reshape(TOTAL, features).astype(jnp.bfloat16)
    grad_values = sums_final[1][margin:].reshape(TOTAL, features).astype(jnp.bfloat16)
    return (layer_out, grad_queries, grad_keys, grad_values, grad_gating)
```

```python
import functools

import jax
import jax.numpy as jnp
from jax import lax
from jax.experimental import pallas as pl
from jax.experimental.pallas import tpu as pltpu
from jax.sharding import PartitionSpec as P

DH = 128
CH = 128
EPSILON = 1e-05
MESH = pl.DeviceIdType.MESH
F32 = jnp.float32
BF16 = jnp.bfloat16


def dot_nt(a, b):
    return lax.dot_general(a, b, (((1,), (1,)), ((), ())), preferred_element_type=F32)


def dot_nn(a, b):
    return lax.dot_general(a, b, (((1,), (0,)), ((), ())), preferred_element_type=F32)


def kernel(
    rows_n, heads_n, factor,
    bounds_h, q_h, k_h, v_h, g_h, c_h,
    lay_o, gq_o, gk_o, gv_o, gg_o,
    bnd, qb, kb, vb, gb, cb,
    k1, v1, k2, v2, q1, q2, d0, d1, d2,
    srel, erel, fq, ft, pt, att, dk, dv, st_out, st_in,
    lsem, s1, r1, s2, r2, sq, rq, sd, rd, ss, rs,
):
    R = q_h.shape[0]
    NC = R // CH
    features = heads_n * DH
    pos = lax.axis_index("rows")
    head = lax.axis_index("heads")
    right = lax.rem(pos + 1, rows_n)
    right2 = lax.rem(pos + 2, rows_n)
    left = lax.rem(pos + rows_n - 1, rows_n)
    left2 = lax.rem(pos + rows_n - 2, rows_n)
    peers = [lax.rem(head + p, heads_n) for p in range(1, heads_n)]

    def sl(c, n=1):
        return pl.ds(c * CH, n * CH)

    barrier = pltpu.get_barrier_semaphore()
    for who in (left, right, right2):
        pl.semaphore_signal(barrier, inc=1, device_id={"rows": who}, device_id_type=MESH)
    for who in peers:
        pl.semaphore_signal(barrier, inc=1, device_id={"heads": who}, device_id_type=MESH)
    loads = [
        pltpu.make_async_copy(src, dst, lsem.at[n])
        for n, (src, dst) in enumerate(
            ((q_h, qb), (k_h, kb), (v_h, vb), (bounds_h, bnd), (g_h, gb), (c_h, cb))
        )
    ]
    for copy in loads:
        copy.start()
    pl.semaphore_wait(barrier, 3 + len(peers))

    def remote(src, dst, send, recv, **who):
        return pltpu.make_async_remote_copy(
            src_ref=src, dst_ref=dst, send_sem=send, recv_sem=recv,
            device_id=who, device_id_type=MESH,
        )

    kv1, kv2 = {}, {}
    for c in reversed(range(NC)):
        kv1[c] = (
            remote(k_h.at[sl(c)], k1.at[sl(c)], s1.at[0, c], r1.at[0, c], rows=right),
            remote(v_h.at[sl(c)], v1.at[sl(c)], s1.at[1, c], r1.at[1, c], rows=right),
        )
        kv2[c] = (
            remote(k1.at[sl(c)], k2.at[sl(c)], s2.at[0, c], r2.at[0, c], rows=right),
            remote(v1.at[sl(c)], v2.at[sl(c)], s2.at[1, c], r2.at[1, c], rows=right),
        )
        for copy in kv1[c]:
            copy.start()
    q_copies = (
        remote(q_h, q1, sq.at[0], rq.at[0], rows=left),
        remote(q_h, q2, sq.at[1], rq.at[1], rows=left2),
    )
    for copy in q_copies:
        copy.start()
    for copy in loads:
        copy.wait()

    first_row = pos * R
    for c in range(NC):
        for row, dst in ((0, srel), (1, erel)):
            line = bnd[row : row + 1, c * CH : (c + 1) * CH] - first_row
            dst[sl(c), :] = jnp.transpose(jnp.broadcast_to(line, (CH, CH)))

    def parts(raw):
        scores = raw * factor
        sigmoid = 1.0 / (1.0 + jnp.exp(-scores))
        return scores * sigmoid, sigmoid * (1.0 + scores * (1.0 - sigmoid))

    def lanes(n, base):
        return lax.broadcasted_iota(jnp.int32, (CH, n * CH), 1) + base

    def wide(column, n):
        return jnp.concatenate([column] * n, axis=1) if n > 1 else column

    def forward(i, off, kk, vv, lo, hi):
        n = hi - lo
        raw = dot_nt(qb[sl(i), :], kk[sl(lo, n), :])
        at = lanes(n, lo * CH - off * R)
        allowed = at >= wide(srel[sl(i), :], n)
        if off == 0:
            rows = lax.broadcasted_iota(jnp.int32, (CH, n * CH), 0) + i * CH
            allowed = allowed & (at <= rows)
        weights, slope = parts(raw)
        fq[off, sl(i), sl(lo, n)] = jnp.where(allowed, slope, 0.0)
        weights = jnp.where(allowed, weights, 0.0).astype(BF16)
        return dot_nn(weights, vv[sl(lo, n), :])

    def prepare(j, off, qq, lo, hi):
        n = hi - lo
        raw = dot_nt(kb[sl(j), :], qq[sl(lo, n), :])
        at = lanes(n, lo * CH + off * R)
        allowed = at <= wide(erel[sl(j), :], n)
        if off == 0:
            keys = lax.broadcasted_iota(jnp.int32, (CH, n * CH), 0) + j * CH
            allowed = allowed & (at >= keys)
        weights, slope = parts(raw)
        ft[off, sl(j), sl(lo, n)] = jnp.where(allowed, slope, 0.0)
        pt[off, sl(j), sl(lo, n)] = jnp.where(allowed, weights, 0.0).astype(BF16)

    for i in range(NC):
        att[sl(i), :] = forward(i, 0, kb, vb, 0, i + 1)
    for j in range(NC):
        prepare(j, 0, qb, j, NC)
    q_copies[0].wait_recv()
    for j in range(NC):
        prepare(j, 1, q1, 0, NC)
    for c in reversed(range(NC)):
        for copy in kv1[c]:
            copy.wait_recv()
        for copy in kv2[c]:
            copy.start()
    for i in range(NC):
        att[sl(i), :] += forward(i, 1, k1, v1, 0, NC)
    q_copies[1].wait_recv()
    for j in range(NC):
        prepare(j, 2, q2, 0, j + 1)

    def stats_copies(c):
        return [
            remote(
                st_out.at[c], st_in.at[head, c], ss.at[p, c], rs.at[head, c], heads=who
            )
            for p, who in enumerate(peers)
        ]

    def stats_send(i):
        rows_t = jnp.transpose(att[sl(i), :])
        scaled_t = jnp.transpose(cb[sl(i), :].astype(F32) * gb[sl(i), :].astype(F32))
        for n, term in enumerate((rows_t, rows_t * rows_t, scaled_t, scaled_t * rows_t)):
            st_out[i, n : n + 1, :] = jnp.sum(term, axis=0, keepdims=True)
        st_in[head, i, 0:4, :] = st_out[i, 0:4, :]
        for copy in stats_copies(i):
            copy.start()

    def stats_use(i):
        for who in peers:
            pltpu.make_async_remote_copy(
                src_ref=st_out.at[i], dst_ref=st_in.at[who, i], send_sem=ss.at[0, i],
                recv_sem=rs.at[who, i], device_id={"heads": who}, device_id_type=MESH,
            ).wait_recv()
        total = st_in[0, i, 0:4, :]
        for p in range(1, heads_n):
            total = total + st_in[p, i, 0:4, :]
        average = total[0:1] / features
        inverse = lax.rsqrt(total[1:2] / features - average * average + EPSILON)
        grad_mean = total[2:3] / features
        cross_mean = inverse * (total[3:4] - average * total[2:3]) / features

        def column(line):
            return jnp.transpose(jnp.broadcast_to(line, (CH, CH)))

        inverse_c = column(inverse)
        normed = (att[sl(i), :] - column(average)) * inverse_c
        gate = gb[sl(i), :].astype(F32)
        upstream = cb[sl(i), :].astype(F32)
        delta = inverse_c * (
            upstream * gate - column(grad_mean) - normed * column(cross_mean)
        )
        d0[sl(i), :] = delta.astype(BF16)
        lay_o[sl(i), :] = (normed * gate).astype(BF16)
        gg_o[sl(i), :] = (upstream * normed).astype(BF16)
        for copy in delta_copies[i]:
            copy.start()

    delta_copies = {
        c: (
            remote(d0.at[sl(c)], d1.at[sl(c)], sd.at[0, c], rd.at[0, c], rows=left),
            remote(d0.at[sl(c)], d2.at[sl(c)], sd.at[1, c], rd.at[1, c], rows=left2),
        )
        for c in range(NC)
    }

    def query_grad(i):
        total = None
        for off, kk, vv, lo, hi in (
            (0, kb, vb, 0, i + 1), (1, k1, v1, 0, NC), (2, k2, v2, i, NC)
        ):
            n = hi - lo
            pulled = dot_nt(d0[sl(i), :], vv[sl(lo, n), :])
            grad = (pulled * fq[off, sl(i), sl(lo, n)]).astype(BF16)
            term = dot_nn(grad, kk[sl(lo, n), :])
            total = term if total is None else total + term
        gq_o[sl(i), :] = (total * factor).astype(BF16)

    def key_grad(i, off, qq, dd, lo, hi, fresh=False):
        n = hi - lo
        delta = dd[sl(i), :]
        pulled = dot_nt(vb[sl(lo, n), :], delta)
        grad = (pulled * ft[off, sl(lo, n), sl(i)]).astype(BF16)
        key_add = dot_nn(grad, qq[sl(i), :])
        value_add = dot_nn(pt[off, sl(lo, n), sl(i)], delta)
        if fresh:
            dk[sl(lo, n), :] = key_add
            dv[sl(lo, n), :] = value_add
        else:
            dk[sl(lo, n), :] += key_add
            dv[sl(lo, n), :] += value_add

    def local_grads(i):
        query_grad(i)
        key_grad(i, 0, qb, d0, 0, i + 1, fresh=i == NC - 1)

    def remote_grads(i):
        delta_copies[i][0].wait_recv()
        key_grad(i, 1, q1, d1, 0, NC)
        delta_copies[i][1].wait_recv()
        key_grad(i, 2, q2, d2, i, NC)

    for c in reversed(range(NC)):
        for copy in kv2[c]:
            copy.wait_recv()
        for i in range(c + 1):
            att[sl(i), :] += forward(i, 2, k2, v2, c, c + 1)
        stats_send(c)
        if c + 1 < NC:
            stats_use(c + 1)
        if c + 2 < NC:
            local_grads(c + 2)
    local_grads(1)
    for i in (3, 2):
        remote_grads(i)
    stats_use(0)
    local_grads(0)
    for i in (1, 0):
        remote_grads(i)
    gk_o[...] = (dk[...] * factor).astype(BF16)
    gv_o[...] = dv[...].astype(BF16)

    for c in range(NC):
        for copy in (*kv1[c], *kv2[c], *delta_copies[c], *stats_copies(c)):
            copy.wait_send()
    for copy in q_copies:
        copy.wait_send()


def local(rows_n, heads_n, queries, key_vectors, value_vectors, gating, bounds, cotangent):
    R, width = queries.shape
    NC = R // CH
    block = (R, width)
    bf = lambda *shape: pltpu.VMEM(shape, BF16)
    fl = lambda *shape: pltpu.VMEM(shape, F32)
    dma = lambda *shape: pltpu.SemaphoreType.DMA(shape)
    out = jax.ShapeDtypeStruct(block, BF16)
    return pl.pallas_call(
        functools.partial(kernel, rows_n, heads_n, DH ** (-0.5)),
        out_shape=(out,) * 5,
        in_specs=[pl.BlockSpec(memory_space=pl.ANY)] * 6,
        out_specs=(pl.BlockSpec(memory_space=pltpu.VMEM),) * 5,
        scratch_shapes=[
            pltpu.VMEM((2, R), jnp.int32),
            *[bf(*block)] * 5,
            *[bf(*block)] * 9,
            pltpu.VMEM((R, CH), jnp.int32), pltpu.VMEM((R, CH), jnp.int32),
            fl(3, R, R), fl(3, R, R), bf(3, R, R),
            fl(*block), fl(*block), fl(*block),
            fl(NC, 8, CH), fl(heads_n, NC, 8, CH),
            dma(6), dma(2, NC), dma(2, NC), dma(2, NC), dma(2, NC),
            dma(2), dma(2), dma(2, NC), dma(2, NC),
            dma(heads_n - 1, NC), dma(heads_n, NC),
        ],
        compiler_params=pltpu.CompilerParams(collective_id=0, has_side_effects=True),
        name="jagged_attention",
    )(bounds, queries, key_vectors, value_vectors, gating, cotangent)


def solution(mesh):
    spec = P("rows", "heads")
    return jax.shard_map(
        functools.partial(local, mesh.shape["rows"], mesh.shape["heads"]),
        mesh=mesh,
        in_specs=(spec, spec, spec, spec, P(None, "rows"), spec),
        out_specs=(spec,) * 5,
        check_vma=False,
    )
```

```python
import functools

import jax
import jax.numpy as jnp
from jax import lax
from jax.experimental import pallas as pl
from jax.experimental.pallas import tpu as pltpu
from jax.sharding import PartitionSpec as P

DH = 128
CH = 128
EPSILON = 1e-05
MESH = pl.DeviceIdType.MESH
F32 = jnp.float32
BF16 = jnp.bfloat16


def dot_nt(a, b):
    return lax.dot_general(a, b, (((1,), (1,)), ((), ())), preferred_element_type=F32)


def dot_nn(a, b):
    return lax.dot_general(a, b, (((1,), (0,)), ((), ())), preferred_element_type=F32)


def kernel(
    rows_n, heads_n, factor,
    bounds_h, q_h, k_h, v_h, g_h, c_h,
    lay_o, gq_o, gk_o, gv_o, gg_o,
    bnd, qb, kb, vb, gb, cb,
    k1, v1, k2, v2, q1, q2, d0, d1, d2,
    srel, erel, fq, ft, pt, att, dk, dv, st_out, st_in,
    lsem, s1, r1, s2, r2, sq, rq, sd, rd, ss, rs,
):
    R = q_h.shape[0]
    NC = R // CH
    features = heads_n * DH
    pos = lax.axis_index("rows")
    head = lax.axis_index("heads")
    right = lax.rem(pos + 1, rows_n)
    right2 = lax.rem(pos + 2, rows_n)
    left = lax.rem(pos + rows_n - 1, rows_n)
    left2 = lax.rem(pos + rows_n - 2, rows_n)
    has_left, has_left2 = pos >= 1, pos >= 2
    has_right, has_right2 = pos < rows_n - 1, pos < rows_n - 2
    peers = [lax.rem(head + p, heads_n) for p in range(1, heads_n)]

    def sl(c, n=1):
        return pl.ds(c * CH, n * CH)

    barrier = pltpu.get_barrier_semaphore()
    for there, who in ((has_left, left), (has_right, right), (has_right2, right2)):
        @pl.when(there)
        def _():
            pl.semaphore_signal(barrier, inc=1, device_id={"rows": who}, device_id_type=MESH)
    for who in peers:
        pl.semaphore_signal(barrier, inc=1, device_id={"heads": who}, device_id_type=MESH)
    loads = [
        pltpu.make_async_copy(src, dst, lsem.at[n])
        for n, (src, dst) in enumerate(
            ((q_h, qb), (k_h, kb), (v_h, vb), (bounds_h, bnd), (g_h, gb), (c_h, cb))
        )
    ]
    for copy in loads:
        copy.start()
    greeters = sum(there.astype(jnp.int32) for there in (has_left, has_left2, has_right))
    pl.semaphore_wait(barrier, greeters + len(peers))

    def remote(src, dst, send, recv, **who):
        return pltpu.make_async_remote_copy(
            src_ref=src, dst_ref=dst, send_sem=send, recv_sem=recv,
            device_id=who, device_id_type=MESH,
        )

    kv1, kv2, delta_copies = {}, {}, {}
    for c in range(NC):
        kv1[c] = (
            remote(k_h.at[sl(c)], k1.at[sl(c)], s1.at[0, c], r1.at[0, c], rows=right),
            remote(v_h.at[sl(c)], v1.at[sl(c)], s1.at[1, c], r1.at[1, c], rows=right),
        )
        kv2[c] = (
            remote(k1.at[sl(c)], k2.at[sl(c)], s2.at[0, c], r2.at[0, c], rows=right),
            remote(v1.at[sl(c)], v2.at[sl(c)], s2.at[1, c], r2.at[1, c], rows=right),
        )
        delta_copies[c] = (
            remote(d0.at[sl(c)], d1.at[sl(c)], sd.at[0, c], rd.at[0, c], rows=left),
            remote(d0.at[sl(c)], d2.at[sl(c)], sd.at[1, c], rd.at[1, c], rows=left2),
        )
    q_copies = (
        remote(q_h, q1, sq.at[0], rq.at[0], rows=left),
        remote(q_h, q2, sq.at[1], rq.at[1], rows=left2),
    )

    @pl.when(has_right)
    def _():
        for c in reversed(range(NC)):
            for copy in kv1[c]:
                copy.start()

    @pl.when(has_left)
    def _():
        q_copies[0].start()

    @pl.when(has_left2)
    def _():
        q_copies[1].start()

    for copy in loads:
        copy.wait()

    first_row = pos * R
    for c in range(NC):
        for row, dst in ((0, srel), (1, erel)):
            line = bnd[row : row + 1, c * CH : (c + 1) * CH] - first_row
            dst[sl(c), :] = jnp.transpose(jnp.broadcast_to(line, (CH, CH)))

    def parts(raw):
        scores = raw * factor
        sigmoid = 1.0 / (1.0 + jnp.exp(-scores))
        return scores * sigmoid, sigmoid * (1.0 + scores * (1.0 - sigmoid))

    def lanes(n, base):
        return lax.broadcasted_iota(jnp.int32, (n * CH, CH), 1) + base

    def sublanes(n, base):
        return lax.broadcasted_iota(jnp.int32, (n * CH, CH), 0) + base

    def forward(c, off, kk, vv, lo, hi, fresh=False):
        n = hi - lo
        raw = dot_nt(qb[sl(lo, n), :], kk[sl(c), :])
        at = lanes(n, c * CH - off * R)
        allowed = at >= srel[sl(lo, n), :]
        if off == 0:
            allowed = allowed & (at <= sublanes(n, lo * CH))
        weights, slope = parts(raw)
        fq[off, c, sl(lo, n), :] = jnp.where(allowed, slope, 0.0)
        weights = jnp.where(allowed, weights, 0.0).astype(BF16)
        term = dot_nn(weights, vv[sl(c), :])
        if fresh:
            att[sl(lo, n), :] = term
        else:
            att[sl(lo, n), :] += term

    def prepare(i, off, qq, lo, hi):
        n = hi - lo
        raw = dot_nt(kb[sl(lo, n), :], qq[sl(i), :])
        at = lanes(n, i * CH + off * R)
        allowed = at <= erel[sl(lo, n), :]
        if off == 0:
            allowed = allowed & (at >= sublanes(n, lo * CH))
        weights, slope = parts(raw)
        ft[off, i, sl(lo, n), :] = jnp.where(allowed, slope, 0.0)
        pt[off, i, sl(lo, n), :] = jnp.where(allowed, weights, 0.0).astype(BF16)

    def stats_copies(c):
        return [
            remote(
                st_out.at[c], st_in.at[head, c], ss.at[p, c], rs.at[head, c], heads=who
            )
            for p, who in enumerate(peers)
        ]

    def stats_send(i):
        rows_t = jnp.transpose(att[sl(i), :])
        scaled_t = jnp.transpose(cb[sl(i), :].astype(F32) * gb[sl(i), :].astype(F32))
        for n, term in enumerate((rows_t, rows_t * rows_t, scaled_t, scaled_t * rows_t)):
            st_out[i, n : n + 1, :] = jnp.sum(term, axis=0, keepdims=True)
        st_in[head, i, 0:4, :] = st_out[i, 0:4, :]
        for copy in stats_copies(i):
            copy.start()

    def stats_use(i):
        for who in peers:
            remote(
                st_out.at[i], st_in.at[who, i], ss.at[0, i], rs.at[who, i], heads=who
            ).wait_recv()
        total = st_in[0, i, 0:4, :]
        for p in range(1, heads_n):
            total = total + st_in[p, i, 0:4, :]
        average = total[0:1] / features
        inverse = lax.rsqrt(total[1:2] / features - average * average + EPSILON)
        grad_mean = total[2:3] / features
        cross_mean = inverse * (total[3:4] - average * total[2:3]) / features

        def column(line):
            return jnp.transpose(jnp.broadcast_to(line, (CH, CH)))

        inverse_c = column(inverse)
        normed = (att[sl(i), :] - column(average)) * inverse_c
        gate = gb[sl(i), :].astype(F32)
        upstream = cb[sl(i), :].astype(F32)
        delta = inverse_c * (
            upstream * gate - column(grad_mean) - normed * column(cross_mean)
        )
        d0[sl(i), :] = delta.astype(BF16)
        lay_o[sl(i), :] = (normed * gate).astype(BF16)
        gg_o[sl(i), :] = (upstream * normed).astype(BF16)

        @pl.when(has_left)
        def _():
            delta_copies[i][0].start()

        @pl.when(has_left2)
        def _():
            delta_copies[i][1].start()

    def query_grad(c, off, kk, vv, lo, hi, fresh=False):
        n = hi - lo
        pulled = dot_nt(d0[sl(lo, n), :], vv[sl(c), :])
        grad = (pulled * fq[off, c, sl(lo, n), :]).astype(BF16)
        term = dot_nn(grad, kk[sl(c), :])
        if fresh:
            att[sl(lo, n), :] = term
        else:
            att[sl(lo, n), :] += term

    def query_grads(lo, hi):
        for c in range(hi):
            query_grad(c, 0, kb, vb, max(lo, c), hi, fresh=c == 0)

        @pl.when(has_left)
        def _():
            for c in range(NC):
                query_grad(c, 1, k1, v1, lo, hi)

        @pl.when(has_left2)
        def _():
            for c in range(lo, NC):
                query_grad(c, 2, k2, v2, lo, min(hi, c + 1))

        gq_o[sl(lo, hi - lo), :] = (att[sl(lo, hi - lo), :] * factor).astype(BF16)

    def key_grad(i, off, qq, dd, lo, hi, fresh=False):
        n = hi - lo
        delta = dd[sl(i), :]
        pulled = dot_nt(vb[sl(lo, n), :], delta)
        grad = (pulled * ft[off, i, sl(lo, n), :]).astype(BF16)
        key_add = dot_nn(grad, qq[sl(i), :])
        value_add = dot_nn(pt[off, i, sl(lo, n), :], delta)
        if fresh:
            dk[sl(lo, n), :] = key_add
            dv[sl(lo, n), :] = value_add
        else:
            dk[sl(lo, n), :] += key_add
            dv[sl(lo, n), :] += value_add

    def remote_grads(i):
        @pl.when(has_right)
        def _():
            delta_copies[i][0].wait_recv()
            key_grad(i, 1, q1, d1, 0, NC)

        @pl.when(has_right2)
        def _():
            delta_copies[i][1].wait_recv()
            key_grad(i, 2, q2, d2, i, NC)

    for c in range(NC):
        forward(c, 0, kb, vb, c, NC, fresh=c == 0)
    for i in range(NC):
        prepare(i, 0, qb, 0, i + 1)
    for c in reversed(range(NC)):
        @pl.when(has_left)
        def _():
            for copy in kv1[c]:
                copy.wait_recv()

            @pl.when(has_right)
            def _():
                for copy in kv2[c]:
                    copy.start()

            forward(c, 1, k1, v1, 0, NC)

    @pl.when(has_right)
    def _():
        q_copies[0].wait_recv()
        for i in range(NC):
            prepare(i, 1, q1, 0, NC)

    @pl.when(has_right2)
    def _():
        q_copies[1].wait_recv()
        for i in range(NC):
            prepare(i, 2, q2, i, NC)

    for c in reversed(range(NC)):
        @pl.when(has_left2)
        def _():
            for copy in kv2[c]:
                copy.wait_recv()
            forward(c, 2, k2, v2, 0, c + 1)

        stats_send(c)
        if c + 1 < NC:
            stats_use(c + 1)
            key_grad(c + 1, 0, qb, d0, 0, c + 2, fresh=c + 1 == NC - 1)
    query_grads(NC // 2, NC)
    for i in reversed(range(NC // 2, NC)):
        remote_grads(i)
    stats_use(0)
    key_grad(0, 0, qb, d0, 0, 1)
    query_grads(0, NC // 2)
    for i in reversed(range(NC // 2)):
        remote_grads(i)
    gk_o[...] = (dk[...] * factor).astype(BF16)
    gv_o[...] = dv[...].astype(BF16)

    @pl.when(has_right)
    def _():
        for c in range(NC):
            for copy in kv1[c]:
                copy.wait_send()

    @pl.when(has_left & has_right)
    def _():
        for c in range(NC):
            for copy in kv2[c]:
                copy.wait_send()

    for n, there in enumerate((has_left, has_left2)):
        @pl.when(there)
        def _():
            q_copies[n].wait_send()
            for c in range(NC):
                delta_copies[c][n].wait_send()

    for c in range(NC):
        for copy in stats_copies(c):
            copy.wait_send()


def store_kernel(*refs):
    sources, results, sems = refs[:5], refs[5:10], refs[10]
    copies = [
        pltpu.make_async_copy(src, dst, sems.at[n])
        for n, (src, dst) in enumerate(zip(sources, results))
    ]
    for copy in copies:
        copy.start()
    for copy in copies:
        copy.wait()


def local(rows_n, heads_n, queries, key_vectors, value_vectors, gating, bounds, cotangent):
    R, width = queries.shape
    NC = R // CH
    block = (R, width)
    bf = lambda *shape: pltpu.VMEM(shape, BF16)
    fl = lambda *shape: pltpu.VMEM(shape, F32)
    dma = lambda *shape: pltpu.SemaphoreType.DMA(shape)
    out = jax.ShapeDtypeStruct(block, BF16)
    held = pl.pallas_call(
        functools.partial(kernel, rows_n, heads_n, DH ** (-0.5)),
        out_shape=(pltpu.VMEM(block, BF16),) * 5,
        in_specs=[pl.BlockSpec(memory_space=pl.ANY)] * 6,
        out_specs=(pl.BlockSpec(memory_space=pltpu.VMEM),) * 5,
        scratch_shapes=[
            pltpu.VMEM((2, R), jnp.int32),
            *[bf(*block)] * 5,
            *[bf(*block)] * 9,
            pltpu.VMEM((R, CH), jnp.int32), pltpu.VMEM((R, CH), jnp.int32),
            fl(3, NC, R, CH), fl(3, NC, R, CH), bf(3, NC, R, CH),
            fl(*block), fl(*block), fl(*block),
            fl(NC, 8, CH), fl(heads_n, NC, 8, CH),
            dma(6), dma(2, NC), dma(2, NC), dma(2, NC), dma(2, NC),
            dma(2), dma(2), dma(2, NC), dma(2, NC),
            dma(heads_n - 1, NC), dma(heads_n, NC),
        ],
        compiler_params=pltpu.CompilerParams(collective_id=0, has_side_effects=True),
        name="jagged_attention",
    )(bounds, queries, key_vectors, value_vectors, gating, cotangent)
    return pl.pallas_call(
        store_kernel,
        out_shape=(out,) * 5,
        in_specs=[pl.BlockSpec(memory_space=pltpu.VMEM)] * 5,
        out_specs=(pl.BlockSpec(memory_space=pl.ANY),) * 5,
        scratch_shapes=[dma(5)],
        name="store_outputs",
    )(*[pltpu.with_memory_space_constraint(x, pltpu.VMEM) for x in held])


def solution(mesh):
    spec = P("rows", "heads")
    return jax.shard_map(
        functools.partial(local, mesh.shape["rows"], mesh.shape["heads"]),
        mesh=mesh,
        in_specs=(spec, spec, spec, spec, P(None, "rows"), spec),
        out_specs=(spec,) * 5,
        check_vma=False,
    )
```

```python
import functools

import jax
import jax.numpy as jnp
from jax import lax
from jax.experimental import pallas as pl
from jax.experimental.pallas import tpu as pltpu
from jax.sharding import PartitionSpec as P

DH = 128
CH = 128
LOG2E = 1.4426950408889634
MASKED = -1e30
EPSILON = 1e-05
MESH = pl.DeviceIdType.MESH
F32 = jnp.float32
BF16 = jnp.bfloat16


def dot_nt(a, b):
    return lax.dot_general(a, b, (((1,), (1,)), ((), ())), preferred_element_type=F32)


def dot_nn(a, b):
    return lax.dot_general(a, b, (((1,), (0,)), ((), ())), preferred_element_type=F32)


def kernel(
    rows_n, heads_n, factor,
    bounds_h, q_h, k_h, v_h, g_h, c_h,
    lay_o, gq_o, gk_o, gv_o, gg_o,
    bnd, qb, kb, vb, gb, cb,
    k1, v1, k2, v2, q1, q2, d0, d1, d2, far, o_out, o_in,
    srel, erel, fq, ft, pt, att, dk, dv, st_out, st_in,
    lsem, s1, r1, s2, r2, so, ro, sq, rq, sd, rd, ss, rs,
):
    R = q_h.shape[0]
    NC = R // CH
    features = heads_n * DH
    pos = lax.axis_index("rows")
    head = lax.axis_index("heads")
    right = lax.rem(pos + 1, rows_n)
    left = lax.rem(pos + rows_n - 1, rows_n)
    has_left, has_left2 = pos >= 1, pos >= 2
    has_right, has_right2 = pos < rows_n - 1, pos < rows_n - 2
    peers = [lax.rem(head + p, heads_n) for p in range(1, heads_n)]

    def sl(c, n=1):
        return pl.ds(c * CH, n * CH)

    barrier = pltpu.get_barrier_semaphore()
    for there, who in ((has_left, left), (has_right, right)):
        @pl.when(there)
        def _():
            pl.semaphore_signal(barrier, inc=1, device_id={"rows": who}, device_id_type=MESH)
    for who in peers:
        pl.semaphore_signal(barrier, inc=1, device_id={"heads": who}, device_id_type=MESH)
    loads = [
        pltpu.make_async_copy(src, dst, lsem.at[n])
        for n, (src, dst) in enumerate(
            ((q_h, qb), (k_h, kb), (v_h, vb), (bounds_h, bnd), (g_h, gb), (c_h, cb))
        )
    ]
    for copy in loads:
        copy.start()
    greeters = has_left.astype(jnp.int32) + has_right.astype(jnp.int32)
    pl.semaphore_wait(barrier, greeters + len(peers))

    def remote(src, dst, send, recv, **who):
        return pltpu.make_async_remote_copy(
            src_ref=src, dst_ref=dst, send_sem=send, recv_sem=recv,
            device_id=who, device_id_type=MESH,
        )

    kv1, kv2, delta_copies = {}, {}, {}
    for c in range(NC):
        kv1[c] = (
            remote(k_h.at[sl(c)], k1.at[sl(c)], s1.at[0, c], r1.at[0, c], rows=right),
            remote(v_h.at[sl(c)], v1.at[sl(c)], s1.at[1, c], r1.at[1, c], rows=right),
        )
        kv2[c] = (
            remote(k1.at[sl(c)], k2.at[sl(c)], s2.at[0, c], r2.at[0, c], rows=right),
            remote(v1.at[sl(c)], v2.at[sl(c)], s2.at[1, c], r2.at[1, c], rows=right),
        )
        delta_copies[c] = (
            remote(d0.at[sl(c)], d1.at[sl(c)], sd.at[0, c], rd.at[0, c], rows=left),
            remote(d1.at[sl(c)], d2.at[sl(c)], sd.at[1, c], rd.at[1, c], rows=left),
        )
    o_copies = [
        remote(o_out.at[sl(c)], o_in.at[sl(c)], so.at[c], ro.at[c], rows=right)
        for c in range(NC)
    ]
    q_copies = (
        remote(q_h, q1, sq.at[0], rq.at[0], rows=left),
        remote(q1, q2, sq.at[1], rq.at[1], rows=left),
    )

    @pl.when(has_right)
    def _():
        for c in reversed(range(NC)):
            for copy in kv1[c]:
                copy.start()

    @pl.when(has_left)
    def _():
        q_copies[0].start()

    for copy in loads:
        copy.wait()

    first_row = pos * R
    for c in range(NC):
        for row, dst in ((0, srel), (1, erel)):
            line = bnd[row : row + 1, c * CH : (c + 1) * CH] - first_row
            dst[sl(c), :] = jnp.transpose(jnp.broadcast_to(line, (CH, CH)))

    def parts(raw, allowed):
        raw = jnp.where(allowed, raw, MASKED)
        scores = raw * factor
        sigmoid = 1.0 / (1.0 + jnp.exp2(raw * (-factor * LOG2E)))
        weights = scores * sigmoid
        return weights, sigmoid * ((1.0 + scores) - weights)

    def lanes(n, base):
        return lax.broadcasted_iota(jnp.int32, (n * CH, CH), 1) + base

    def sublanes(n, base):
        return lax.broadcasted_iota(jnp.int32, (n * CH, CH), 0) + base

    def halves(value, w):
        return [value[:, m * CH : (m + 1) * CH] for m in range(w)]

    def joined(values):
        return values[0] if len(values) == 1 else jnp.concatenate(values, axis=1)

    def forward(c, w, off, kk, vv, lo, hi, fresh=False):
        n = hi - lo
        packed = []
        for m, raw in enumerate(halves(dot_nt(qb[sl(lo, n), :], kk[sl(c, w), :]), w)):
            at = lanes(n, (c + m) * CH - off * R)
            allowed = at >= srel[sl(lo, n), :]
            if off == 0:
                allowed = allowed & (at <= sublanes(n, lo * CH))
            weights, slope = parts(raw, allowed)
            fq[off, c + m, sl(lo, n), :] = slope
            packed.append(weights.astype(BF16))
        term = dot_nn(joined(packed), vv[sl(c, w), :])
        if fresh:
            att[sl(lo, n), :] = term
        else:
            att[sl(lo, n), :] += term

    def bridge(c, w, hi):
        first, last = srel[R - 1 : R, :], erel[R - 1 : R, :]
        packed = []
        for m, raw in enumerate(halves(dot_nt(q1[sl(0, hi), :], k1[sl(c, w), :]), w)):
            allowed = (lanes(hi, (c + m) * CH - R) >= first) & (sublanes(hi, R) <= last)
            packed.append(parts(raw, allowed)[0].astype(BF16))
        term = dot_nn(joined(packed), v1[sl(c, w), :])
        if hi == NC:
            far[...] = term
        else:
            far[sl(0, hi), :] += term
        for i in reversed(range(c, hi)):
            o_out[sl(i), :] = far[sl(i), :].astype(BF16)
            o_copies[i].start()

    def far_slopes(c, w, hi):
        for m, raw in enumerate(halves(dot_nt(qb[sl(0, hi), :], k2[sl(c, w), :]), w)):
            allowed = lanes(hi, (c + m) * CH - 2 * R) >= srel[sl(0, hi), :]
            fq[2, c + m, sl(0, hi), :] = parts(raw, allowed)[1]

    def prepare(i, w, off, qq, lo, hi):
        n = hi - lo
        for m, raw in enumerate(halves(dot_nt(kb[sl(lo, n), :], qq[sl(i, w), :]), w)):
            at = lanes(n, (i + m) * CH + off * R)
            allowed = at <= erel[sl(lo, n), :]
            if off == 0:
                allowed = allowed & (at >= sublanes(n, lo * CH))
            weights, slope = parts(raw, allowed)
            ft[off, i + m, sl(lo, n), :] = slope
            pt[off, i + m, sl(lo, n), :] = weights.astype(BF16)

    def stats_copies(c):
        return [
            remote(
                st_out.at[c], st_in.at[head, c], ss.at[p, c], rs.at[head, c], heads=who
            )
            for p, who in enumerate(peers)
        ]

    def stats_send(i):
        rows_t = jnp.transpose(att[sl(i), :])
        scaled_t = jnp.transpose(cb[sl(i), :].astype(F32) * gb[sl(i), :].astype(F32))
        for n, term in enumerate((rows_t, rows_t * rows_t, scaled_t, scaled_t * rows_t)):
            st_out[i, n : n + 1, :] = jnp.sum(term, axis=0, keepdims=True)
        st_in[head, i, 0:4, :] = st_out[i, 0:4, :]
        for copy in stats_copies(i):
            copy.start()

    def stats_use(i):
        for who in peers:
            remote(
                st_out.at[i], st_in.at[who, i], ss.at[0, i], rs.at[who, i], heads=who
            ).wait_recv()
        total = st_in[0, i, 0:4, :]
        for p in range(1, heads_n):
            total = total + st_in[p, i, 0:4, :]
        average = total[0:1] / features
        inverse = lax.rsqrt(total[1:2] / features - average * average + EPSILON)
        grad_mean = total[2:3] / features
        cross_mean = inverse * (total[3:4] - average * total[2:3]) / features

        def column(line):
            return jnp.transpose(jnp.broadcast_to(line, (CH, CH)))

        inverse_c = column(inverse)
        normed = (att[sl(i), :] - column(average)) * inverse_c
        gate = gb[sl(i), :].astype(F32)
        upstream = cb[sl(i), :].astype(F32)
        delta = inverse_c * (
            upstream * gate - column(grad_mean) - normed * column(cross_mean)
        )
        d0[sl(i), :] = delta.astype(BF16)
        lay_o[sl(i), :] = (normed * gate).astype(BF16)
        gg_o[sl(i), :] = (upstream * normed).astype(BF16)

        @pl.when(has_left)
        def _():
            delta_copies[i][0].start()

    def query_grad(c, off, kk, vv, lo, hi, fresh=False):
        n = hi - lo
        pulled = dot_nt(d0[sl(lo, n), :], vv[sl(c, 2), :])
        slope = joined([fq[off, c + m, sl(lo, n), :] for m in range(2)])
        term = dot_nn((pulled * slope).astype(BF16), kk[sl(c, 2), :])
        if fresh:
            att[sl(lo, n), :] = term
        else:
            att[sl(lo, n), :] += term

    def query_grads():
        query_grad(0, 0, kb, vb, 0, NC, fresh=True)
        query_grad(2, 0, kb, vb, 2, NC)

        @pl.when(has_left)
        def _():
            query_grad(0, 1, k1, v1, 0, NC)
            query_grad(2, 1, k1, v1, 0, NC)

        @pl.when(has_left2)
        def _():
            query_grad(0, 2, k2, v2, 0, 2)
            query_grad(2, 2, k2, v2, 0, NC)

        gq_o[...] = (att[...] * factor).astype(BF16)

    def key_grad(i, off, qq, dd, lo, hi, fresh=False):
        n = hi - lo
        delta = dd[sl(i, 2), :]
        pulled = dot_nt(vb[sl(lo, n), :], delta)
        slope = joined([ft[off, i + m, sl(lo, n), :] for m in range(2)])
        key_add = dot_nn((pulled * slope).astype(BF16), qq[sl(i, 2), :])
        weights = joined([pt[off, i + m, sl(lo, n), :] for m in range(2)])
        value_add = dot_nn(weights, delta)
        if fresh:
            dk[sl(lo, n), :] = key_add
            dv[sl(lo, n), :] = value_add
        else:
            dk[sl(lo, n), :] += key_add
            dv[sl(lo, n), :] += value_add

    def relay(i):
        @pl.when(has_right)
        def _():
            delta_copies[i][0].wait_recv()

            @pl.when(has_left)
            def _():
                delta_copies[i][1].start()

    def near_grad(i):
        @pl.when(has_right)
        def _():
            key_grad(i, 1, q1, d1, 0, NC)

    def far_grad(i):
        @pl.when(has_right2)
        def _():
            for c in (i, i + 1):
                delta_copies[c][1].wait_recv()
            key_grad(i, 2, q2, d2, i, NC)

    def arrive(c):
        @pl.when(has_left2)
        def _():
            o_copies[c].wait_recv()
            att[sl(c), :] += o_in[sl(c), :].astype(F32)

        stats_send(c)

    def far_arrive():
        @pl.when(has_left2)
        def _():
            for c in reversed(range(NC)):
                for copy in kv2[c]:
                    copy.wait_recv()
            far_slopes(2, 2, NC)
            far_slopes(0, 2, 2)

    forward(0, 2, 0, kb, vb, 0, NC, fresh=True)
    forward(2, 2, 0, kb, vb, 2, NC)
    prepare(0, 2, 0, qb, 0, 2)
    prepare(2, 2, 0, qb, 0, NC)

    @pl.when(has_right)
    def _():
        q_copies[0].wait_recv()

        @pl.when(has_left)
        def _():
            q_copies[1].start()

    for c, w in ((2, 2), (1, 1), (0, 1)):
        @pl.when(has_left)
        def _():
            for m in range(w):
                for copy in kv1[c + m]:
                    copy.wait_recv()

            @pl.when(has_right)
            def _():
                bridge(c, w, c + w)

            forward(c, w, 1, k1, v1, 0, NC)

    @pl.when(has_left & has_right)
    def _():
        for c in reversed(range(NC)):
            for copy in kv2[c]:
                copy.start()

    for c in reversed(range(NC)):
        arrive(c)

    @pl.when(has_right)
    def _():
        prepare(0, 2, 1, q1, 0, NC)
        prepare(2, 2, 1, q1, 0, NC)

    @pl.when(has_right2)
    def _():
        q_copies[1].wait_recv()
        prepare(0, 2, 2, q2, 0, NC)
        prepare(2, 2, 2, q2, 2, NC)

    for c in reversed(range(NC)):
        stats_use(c)
    relay(3)
    key_grad(2, 0, qb, d0, 0, NC, fresh=True)
    relay(2)
    key_grad(0, 0, qb, d0, 0, 2)
    relay(1)
    near_grad(2)
    relay(0)
    near_grad(0)
    far_arrive()
    query_grads()
    far_grad(2)
    far_grad(0)
    gk_o[...] = (dk[...] * factor).astype(BF16)
    gv_o[...] = dv[...].astype(BF16)

    @pl.when(has_right)
    def _():
        for c in range(NC):
            for copy in kv1[c]:
                copy.wait_send()

    @pl.when(has_left & has_right)
    def _():
        for c in range(NC):
            o_copies[c].wait_send()
            for copy in kv2[c]:
                copy.wait_send()

    @pl.when(has_left)
    def _():
        q_copies[0].wait_send()
        for c in range(NC):
            delta_copies[c][0].wait_send()

    @pl.when(has_left & has_right)
    def _():
        q_copies[1].wait_send()
        for c in range(NC):
            delta_copies[c][1].wait_send()

    for c in range(NC):
        for copy in stats_copies(c):
            copy.wait_send()


def store_kernel(*refs):
    sources, results, sems = refs[:5], refs[5:10], refs[10]
    copies = [
        pltpu.make_async_copy(src, dst, sems.at[n])
        for n, (src, dst) in enumerate(zip(sources, results))
    ]
    for copy in copies:
        copy.start()
    for copy in copies:
        copy.wait()


def local(rows_n, heads_n, queries, key_vectors, value_vectors, gating, bounds, cotangent):
    R, width = queries.shape
    NC = R // CH
    block = (R, width)
    bf = lambda *shape: pltpu.VMEM(shape, BF16)
    fl = lambda *shape: pltpu.VMEM(shape, F32)
    dma = lambda *shape: pltpu.SemaphoreType.DMA(shape)
    out = jax.ShapeDtypeStruct(block, BF16)
    held = pl.pallas_call(
        functools.partial(kernel, rows_n, heads_n, DH ** (-0.5)),
        out_shape=(pltpu.VMEM(block, BF16),) * 5,
        in_specs=[pl.BlockSpec(memory_space=pl.ANY)] * 6,
        out_specs=(pl.BlockSpec(memory_space=pltpu.VMEM),) * 5,
        scratch_shapes=[
            pltpu.VMEM((2, R), jnp.int32),
            *[bf(*block)] * 5,
            *[bf(*block)] * 9,
            fl(*block), bf(*block), bf(*block),
            pltpu.VMEM((R, CH), jnp.int32), pltpu.VMEM((R, CH), jnp.int32),
            fl(3, NC, R, CH), fl(3, NC, R, CH), bf(3, NC, R, CH),
            fl(*block), fl(*block), fl(*block),
            fl(NC, 8, CH), fl(heads_n, NC, 8, CH),
            dma(6), dma(2, NC), dma(2, NC), dma(2, NC), dma(2, NC), dma(NC), dma(NC),
            dma(2), dma(2), dma(2, NC), dma(2, NC),
            dma(heads_n - 1, NC), dma(heads_n, NC),
        ],
        compiler_params=pltpu.CompilerParams(collective_id=0, has_side_effects=True),
        name="jagged_attention",
    )(bounds, queries, key_vectors, value_vectors, gating, cotangent)
    return pl.pallas_call(
        store_kernel,
        out_shape=(out,) * 5,
        in_specs=[pl.BlockSpec(memory_space=pltpu.VMEM)] * 5,
        out_specs=(pl.BlockSpec(memory_space=pl.ANY),) * 5,
        scratch_shapes=[dma(5)],
        name="store_outputs",
    )(*[pltpu.with_memory_space_constraint(x, pltpu.VMEM) for x in held])


def solution(mesh):
    spec = P("rows", "heads")
    return jax.shard_map(
        functools.partial(local, mesh.shape["rows"], mesh.shape["heads"]),
        mesh=mesh,
        in_specs=(spec, spec, spec, spec, P(None, "rows"), spec),
        out_specs=(spec,) * 5,
        check_vma=False,
    )
```

```python
import functools

import jax
import jax.numpy as jnp
from jax import lax
from jax.experimental import pallas as pl
from jax.experimental.pallas import tpu as pltpu
from jax.sharding import PartitionSpec as P

DH = 128
CH = 128
USHER = 2
LAZY = (1,)
LOG2E = 1.4426950408889634
MASKED = -1e30
EPSILON = 1e-05
MESH = pl.DeviceIdType.MESH
F32 = jnp.float32
BF16 = jnp.bfloat16


def dot_nt(a, b):
    return lax.dot_general(a, b, (((1,), (1,)), ((), ())), preferred_element_type=F32)


def dot_nn(a, b):
    return lax.dot_general(a, b, (((1,), (0,)), ((), ())), preferred_element_type=F32)


def kernel(
    rows_n, heads_n, factor,
    bounds_h, q_h, k_h, v_h, g_h, c_h,
    lay_o, gq_o, gk_o, gv_o, gg_o,
    bnd, qb, kb, vb, gb, cb,
    k1, v1, k2, v2, q1, q2, d0, d1, d2, far, o_out, o_in,
    srel, erel, fq, ft, pt, att, dk, dv, st_out, st_in,
    lsem, s1, r1, s2, r2, so, ro, sq, rq, sd, rd, ss, rs, usher_sem, left_sem,
):
    R = q_h.shape[0]
    NC = R // CH
    features = heads_n * DH
    pos = lax.axis_index("rows")
    head = lax.axis_index("heads")
    right = lax.rem(pos + 1, rows_n)
    left = lax.rem(pos + rows_n - 1, rows_n)
    has_left, has_left2 = pos >= 1, pos >= 2
    has_right, has_right2 = pos < rows_n - 1, pos < rows_n - 2
    peers = [lax.rem(head + p, heads_n) for p in range(1, heads_n)]

    def sl(c, n=1):
        return pl.ds(c * CH, n * CH)

    lazy_left = functools.reduce(jnp.logical_or, [pos == row for row in LAZY])
    lazy_right = functools.reduce(jnp.logical_or, [pos == row - 1 for row in LAZY])
    barrier = pltpu.get_barrier_semaphore()
    for there, who in ((has_left, left), (has_right & ~lazy_right, right)):
        @pl.when(there)
        def _():
            pl.semaphore_signal(barrier, inc=1, device_id={"rows": who}, device_id_type=MESH)

    for who in peers:
        @pl.when((head != 0) | (who == USHER))
        def _():
            pl.semaphore_signal(barrier, inc=1, device_id={"heads": who}, device_id_type=MESH)
    loads = [
        pltpu.make_async_copy(src, dst, lsem.at[n])
        for n, (src, dst) in enumerate(
            ((q_h, qb), (k_h, kb), (v_h, vb), (bounds_h, bnd), (g_h, gb), (c_h, cb))
        )
    ]
    for copy in loads:
        copy.start()
    greeters = has_right.astype(jnp.int32) + (has_left & ~lazy_left).astype(jnp.int32)
    ushered = (head != 0) & (head != USHER)
    pl.semaphore_wait(barrier, greeters + len(peers) - ushered.astype(jnp.int32))

    def remote(src, dst, send, recv, **who):
        return pltpu.make_async_remote_copy(
            src_ref=src, dst_ref=dst, send_sem=send, recv_sem=recv,
            device_id=who, device_id_type=MESH,
        )

    kv1, kv2, delta_copies = {}, {}, {}
    for c in range(NC):
        kv1[c] = (
            remote(k_h.at[sl(c)], k1.at[sl(c)], s1.at[0, c], r1.at[0, c], rows=right),
            remote(v_h.at[sl(c)], v1.at[sl(c)], s1.at[1, c], r1.at[1, c], rows=right),
        )
        kv2[c] = (
            remote(k1.at[sl(c)], k2.at[sl(c)], s2.at[0, c], r2.at[0, c], rows=right),
            remote(v1.at[sl(c)], v2.at[sl(c)], s2.at[1, c], r2.at[1, c], rows=right),
        )
        delta_copies[c] = (
            remote(d0.at[sl(c)], d1.at[sl(c)], sd.at[0, c], rd.at[0, c], rows=left),
            remote(d1.at[sl(c)], d2.at[sl(c)], sd.at[1, c], rd.at[1, c], rows=left),
        )
    o_copies = [
        remote(o_out.at[sl(c)], o_in.at[sl(c)], so.at[c], ro.at[c], rows=right)
        for c in range(NC)
    ]
    q_copies = (
        remote(q_h, q1, sq.at[0], rq.at[0], rows=left),
        remote(q1, q2, sq.at[1], rq.at[1], rows=left),
    )

    @pl.when(has_right)
    def _():
        for c in reversed(range(NC)):
            for copy in kv1[c]:
                copy.start()

    @pl.when(lazy_right)
    def _():
        pl.semaphore_signal(left_sem, inc=1, device_id={"rows": right}, device_id_type=MESH)

    @pl.when(head == USHER)
    def _():
        for who in peers:
            @pl.when(who != 0)
            def _():
                pl.semaphore_signal(usher_sem, inc=1, device_id={"heads": who}, device_id_type=MESH)

    @pl.when(lazy_left)
    def _():
        pl.semaphore_wait(left_sem, 1)

    @pl.when(has_left)
    def _():
        q_copies[0].start()

    for copy in loads:
        copy.wait()

    first_row = pos * R
    for c in range(NC):
        for row, dst in ((0, srel), (1, erel)):
            line = bnd[row : row + 1, c * CH : (c + 1) * CH] - first_row
            dst[sl(c), :] = jnp.transpose(jnp.broadcast_to(line, (CH, CH)))

    def parts(raw, allowed):
        raw = jnp.where(allowed, raw, MASKED)
        scores = raw * factor
        sigmoid = 1.0 / (1.0 + jnp.exp2(raw * (-factor * LOG2E)))
        weights = scores * sigmoid
        return weights, sigmoid * ((1.0 + scores) - weights)

    def lanes(n, base):
        return lax.broadcasted_iota(jnp.int32, (n * CH, CH), 1) + base

    def sublanes(n, base):
        return lax.broadcasted_iota(jnp.int32, (n * CH, CH), 0) + base

    def halves(value, w):
        return [value[:, m * CH : (m + 1) * CH] for m in range(w)]

    def joined(values):
        return values[0] if len(values) == 1 else jnp.concatenate(values, axis=1)

    def forward(c, w, off, kk, vv, lo, hi, fresh=False):
        n = hi - lo
        packed = []
        for m, raw in enumerate(halves(dot_nt(qb[sl(lo, n), :], kk[sl(c, w), :]), w)):
            at = lanes(n, (c + m) * CH - off * R)
            allowed = at >= srel[sl(lo, n), :]
            if off == 0:
                allowed = allowed & (at <= sublanes(n, lo * CH))
            weights, slope = parts(raw, allowed)
            fq[off, c + m, sl(lo, n), :] = slope
            packed.append(weights.astype(BF16))
        term = dot_nn(joined(packed), vv[sl(c, w), :])
        if fresh:
            att[sl(lo, n), :] = term
        else:
            att[sl(lo, n), :] += term

    def bridge(c, w, hi):
        first, last = srel[R - 1 : R, :], erel[R - 1 : R, :]
        packed = []
        for m, raw in enumerate(halves(dot_nt(q1[sl(0, hi), :], k1[sl(c, w), :]), w)):
            allowed = (lanes(hi, (c + m) * CH - R) >= first) & (sublanes(hi, R) <= last)
            packed.append(parts(raw, allowed)[0].astype(BF16))
        term = dot_nn(joined(packed), v1[sl(c, w), :])
        if hi == NC:
            far[...] = term
        else:
            far[sl(0, hi), :] += term
        for i in reversed(range(c, hi)):
            o_out[sl(i), :] = far[sl(i), :].astype(BF16)
            o_copies[i].start()

    def far_slopes(c, w, hi):
        for m, raw in enumerate(halves(dot_nt(qb[sl(0, hi), :], k2[sl(c, w), :]), w)):
            allowed = lanes(hi, (c + m) * CH - 2 * R) >= srel[sl(0, hi), :]
            fq[2, c + m, sl(0, hi), :] = parts(raw, allowed)[1]

    def prepare(i, w, off, qq, lo, hi):
        n = hi - lo
        for m, raw in enumerate(halves(dot_nt(kb[sl(lo, n), :], qq[sl(i, w), :]), w)):
            at = lanes(n, (i + m) * CH + off * R)
            allowed = at <= erel[sl(lo, n), :]
            if off == 0:
                allowed = allowed & (at >= sublanes(n, lo * CH))
            weights, slope = parts(raw, allowed)
            ft[off, i + m, sl(lo, n), :] = slope
            pt[off, i + m, sl(lo, n), :] = weights.astype(BF16)

    def stats_copies(c):
        return [
            remote(
                st_out.at[c], st_in.at[head, c], ss.at[p, c], rs.at[head, c], heads=who
            )
            for p, who in enumerate(peers)
        ]

    def stats_send(i):
        rows_t = jnp.transpose(att[sl(i), :])
        scaled_t = jnp.transpose(cb[sl(i), :].astype(F32) * gb[sl(i), :].astype(F32))
        for n, term in enumerate((rows_t, rows_t * rows_t, scaled_t, scaled_t * rows_t)):
            st_out[i, n : n + 1, :] = jnp.sum(term, axis=0, keepdims=True)
        st_in[head, i, 0:4, :] = st_out[i, 0:4, :]
        for copy in stats_copies(i):
            copy.start()

    def stats_use(i):
        for who in peers:
            remote(
                st_out.at[i], st_in.at[who, i], ss.at[0, i], rs.at[who, i], heads=who
            ).wait_recv()
        total = st_in[0, i, 0:4, :]
        for p in range(1, heads_n):
            total = total + st_in[p, i, 0:4, :]
        average = total[0:1] / features
        inverse = lax.rsqrt(total[1:2] / features - average * average + EPSILON)
        grad_mean = total[2:3] / features
        cross_mean = inverse * (total[3:4] - average * total[2:3]) / features

        def column(line):
            return jnp.transpose(jnp.broadcast_to(line, (CH, CH)))

        inverse_c = column(inverse)
        normed = (att[sl(i), :] - column(average)) * inverse_c
        gate = gb[sl(i), :].astype(F32)
        upstream = cb[sl(i), :].astype(F32)
        delta = inverse_c * (
            upstream * gate - column(grad_mean) - normed * column(cross_mean)
        )
        d0[sl(i), :] = delta.astype(BF16)
        lay_o[sl(i), :] = (normed * gate).astype(BF16)
        gg_o[sl(i), :] = (upstream * normed).astype(BF16)

        @pl.when(has_left)
        def _():
            delta_copies[i][0].start()

    def query_grad(c, off, kk, vv, lo, hi, fresh=False):
        n = hi - lo
        pulled = dot_nt(d0[sl(lo, n), :], vv[sl(c, 2), :])
        slope = joined([fq[off, c + m, sl(lo, n), :] for m in range(2)])
        term = dot_nn((pulled * slope).astype(BF16), kk[sl(c, 2), :])
        if fresh:
            att[sl(lo, n), :] = term
        else:
            att[sl(lo, n), :] += term

    def query_own():
        query_grad(0, 0, kb, vb, 0, NC, fresh=True)
        query_grad(2, 0, kb, vb, 2, NC)

    def query_far():
        @pl.when(has_left)
        def _():
            query_grad(0, 1, k1, v1, 0, NC)
            query_grad(2, 1, k1, v1, 0, NC)

        @pl.when(has_left2)
        def _():
            query_grad(0, 2, k2, v2, 0, 2)
            query_grad(2, 2, k2, v2, 0, NC)

        gq_o[...] = (att[...] * factor).astype(BF16)

    def key_grad(i, off, qq, dd, lo, hi, fresh=False):
        n = hi - lo
        delta = dd[sl(i, 2), :]
        pulled = dot_nt(vb[sl(lo, n), :], delta)
        slope = joined([ft[off, i + m, sl(lo, n), :] for m in range(2)])
        key_add = dot_nn((pulled * slope).astype(BF16), qq[sl(i, 2), :])
        weights = joined([pt[off, i + m, sl(lo, n), :] for m in range(2)])
        value_add = dot_nn(weights, delta)
        if fresh:
            dk[sl(lo, n), :] = key_add
            dv[sl(lo, n), :] = value_add
        else:
            dk[sl(lo, n), :] += key_add
            dv[sl(lo, n), :] += value_add

    def relay(i):
        @pl.when(has_right)
        def _():
            delta_copies[i][0].wait_recv()

            @pl.when(has_left)
            def _():
                delta_copies[i][1].start()

    def near_grad(i):
        @pl.when(has_right)
        def _():
            key_grad(i, 1, q1, d1, 0, NC)

    def far_grad(i):
        @pl.when(has_right2)
        def _():
            for c in (i, i + 1):
                delta_copies[c][1].wait_recv()
            key_grad(i, 2, q2, d2, i, NC)

    def arrive(c):
        @pl.when(has_left2)
        def _():
            o_copies[c].wait_recv()
            att[sl(c), :] += o_in[sl(c), :].astype(F32)

        stats_send(c)

    def far_arrive():
        @pl.when(has_left2)
        def _():
            for c in reversed(range(NC)):
                for copy in kv2[c]:
                    copy.wait_recv()
            far_slopes(2, 2, NC)
            far_slopes(0, 2, 2)

    forward(0, 2, 0, kb, vb, 0, NC, fresh=True)
    forward(2, 2, 0, kb, vb, 2, NC)
    prepare(0, 2, 0, qb, 0, 2)
    prepare(2, 2, 0, qb, 0, NC)

    @pl.when(has_right)
    def _():
        q_copies[0].wait_recv()

        @pl.when(has_left)
        def _():
            q_copies[1].start()

    for c, w in ((2, 2), (1, 1), (0, 1)):
        @pl.when(has_left)
        def _():
            for m in range(w):
                for copy in kv1[c + m]:
                    copy.wait_recv()

            @pl.when(has_right)
            def _():
                bridge(c, w, c + w)

            forward(c, w, 1, k1, v1, 0, NC)

    @pl.when(has_left & has_right)
    def _():
        for c in reversed(range(NC)):
            for copy in kv2[c]:
                copy.start()

    @pl.when(ushered)
    def _():
        pl.semaphore_wait(usher_sem, 1)

    for c in reversed(range(NC)):
        arrive(c)

    @pl.when(has_right)
    def _():
        prepare(0, 2, 1, q1, 0, NC)
        prepare(2, 2, 1, q1, 0, NC)

    @pl.when(has_right2)
    def _():
        q_copies[1].wait_recv()
        prepare(0, 2, 2, q2, 0, NC)
        prepare(2, 2, 2, q2, 2, NC)

    for c in reversed(range(NC)):
        stats_use(c)
    key_grad(2, 0, qb, d0, 0, NC, fresh=True)
    relay(3)
    query_own()
    relay(2)
    key_grad(0, 0, qb, d0, 0, 2)
    relay(1)
    near_grad(2)
    relay(0)
    near_grad(0)
    far_arrive()
    query_far()
    far_grad(2)
    far_grad(0)
    gk_o[...] = (dk[...] * factor).astype(BF16)
    gv_o[...] = dv[...].astype(BF16)

    @pl.when(has_right)
    def _():
        for c in range(NC):
            for copy in kv1[c]:
                copy.wait_send()

    @pl.when(has_left & has_right)
    def _():
        for c in range(NC):
            o_copies[c].wait_send()
            for copy in kv2[c]:
                copy.wait_send()

    @pl.when(has_left)
    def _():
        q_copies[0].wait_send()
        for c in range(NC):
            delta_copies[c][0].wait_send()

    @pl.when(has_left & has_right)
    def _():
        q_copies[1].wait_send()
        for c in range(NC):
            delta_copies[c][1].wait_send()

    for c in range(NC):
        for copy in stats_copies(c):
            copy.wait_send()


def store_kernel(*refs):
    sources, results, sems = refs[:5], refs[5:10], refs[10]
    copies = [
        pltpu.make_async_copy(src, dst, sems.at[n])
        for n, (src, dst) in enumerate(zip(sources, results))
    ]
    for copy in copies:
        copy.start()
    for copy in copies:
        copy.wait()


def local(rows_n, heads_n, queries, key_vectors, value_vectors, gating, bounds, cotangent):
    R, width = queries.shape
    NC = R // CH
    block = (R, width)
    bf = lambda *shape: pltpu.VMEM(shape, BF16)
    fl = lambda *shape: pltpu.VMEM(shape, F32)
    dma = lambda *shape: pltpu.SemaphoreType.DMA(shape)
    out = jax.ShapeDtypeStruct(block, BF16)
    held = pl.pallas_call(
        functools.partial(kernel, rows_n, heads_n, DH ** (-0.5)),
        out_shape=(pltpu.VMEM(block, BF16),) * 5,
        in_specs=[pl.BlockSpec(memory_space=pl.ANY)] * 6,
        out_specs=(pl.BlockSpec(memory_space=pltpu.VMEM),) * 5,
        scratch_shapes=[
            pltpu.VMEM((2, R), jnp.int32),
            *[bf(*block)] * 5,
            *[bf(*block)] * 9,
            fl(*block), bf(*block), bf(*block),
            pltpu.VMEM((R, CH), jnp.int32), pltpu.VMEM((R, CH), jnp.int32),
            fl(3, NC, R, CH), fl(3, NC, R, CH), bf(3, NC, R, CH),
            fl(*block), fl(*block), fl(*block),
            fl(NC, 8, CH), fl(heads_n, NC, 8, CH),
            dma(6), dma(2, NC), dma(2, NC), dma(2, NC), dma(2, NC), dma(NC), dma(NC),
            dma(2), dma(2), dma(2, NC), dma(2, NC),
            dma(heads_n - 1, NC), dma(heads_n, NC), pltpu.SemaphoreType.REGULAR, pltpu.SemaphoreType.REGULAR,
        ],
        compiler_params=pltpu.CompilerParams(collective_id=0, has_side_effects=True),
        name="jagged_attention",
    )(bounds, queries, key_vectors, value_vectors, gating, cotangent)
    return pl.pallas_call(
        store_kernel,
        out_shape=(out,) * 5,
        in_specs=[pl.BlockSpec(memory_space=pltpu.VMEM)] * 5,
        out_specs=(pl.BlockSpec(memory_space=pl.ANY),) * 5,
        scratch_shapes=[dma(5)],
        name="store_outputs",
    )(*[pltpu.with_memory_space_constraint(x, pltpu.VMEM) for x in held])


def solution(mesh):
    spec = P("rows", "heads")
    return jax.shard_map(
        functools.partial(local, mesh.shape["rows"], mesh.shape["heads"]),
        mesh=mesh,
        in_specs=(spec, spec, spec, spec, P(None, "rows"), spec),
        out_specs=(spec,) * 5,
        check_vma=False,
    )
```

```python
import functools

import jax
import jax.numpy as jnp
from jax import lax
from jax.experimental import pallas as pl
from jax.experimental.pallas import tpu as pltpu
from jax.sharding import PartitionSpec as P

DH = 128
CH = 128
USHER = 2
LAZY = (1,)
LOG2E = 1.4426950408889634
MASKED = -1e30
EPSILON = 1e-05
MESH = pl.DeviceIdType.MESH
F32 = jnp.float32
BF16 = jnp.bfloat16


def dot_nt(a, b):
    return lax.dot_general(a, b, (((1,), (1,)), ((), ())), preferred_element_type=F32)


def dot_nn(a, b):
    return lax.dot_general(a, b, (((1,), (0,)), ((), ())), preferred_element_type=F32)


def kernel(
    rows_n, heads_n, factor,
    bounds_h, q_h, k_h, v_h, g_h, c_h,
    lay_o, gq_o, gk_o, gv_o, gg_o,
    bnd, qb, kb, vb, gb, cb,
    k1, v1, k2, v2, q1, q2, d0, d1, d2, far, o_out, o_in,
    srel, erel, fq, ft, pt, att, dk, dv, st_out, st_in,
    lsem, s1, r1, s2, r2, so, ro, sq, rq, sd, rd, ss, rs, usher_sem, left_sem,
):
    R = q_h.shape[0]
    NC = R // CH
    features = heads_n * DH
    pos = lax.axis_index("rows")
    head = lax.axis_index("heads")
    right = lax.rem(pos + 1, rows_n)
    left = lax.rem(pos + rows_n - 1, rows_n)
    has_left, has_left2 = pos >= 1, pos >= 2
    has_right, has_right2 = pos < rows_n - 1, pos < rows_n - 2
    peers = [lax.rem(head + p, heads_n) for p in range(1, heads_n)]

    def sl(c, n=1):
        return pl.ds(c * CH, n * CH)

    lazy_left = functools.reduce(jnp.logical_or, [pos == row for row in LAZY])
    lazy_right = functools.reduce(jnp.logical_or, [pos == row - 1 for row in LAZY])
    barrier = pltpu.get_barrier_semaphore()
    for there, who in ((has_left, left), (has_right & ~lazy_right, right)):
        @pl.when(there)
        def _():
            pl.semaphore_signal(barrier, inc=1, device_id={"rows": who}, device_id_type=MESH)

    for who in peers:
        @pl.when((head != 0) | (who == USHER))
        def _():
            pl.semaphore_signal(barrier, inc=1, device_id={"heads": who}, device_id_type=MESH)
    loads = [
        pltpu.make_async_copy(src, dst, lsem.at[n])
        for n, (src, dst) in enumerate(
            ((q_h, qb), (k_h, kb), (v_h, vb), (bounds_h, bnd), (g_h, gb), (c_h, cb))
        )
    ]
    for copy in loads:
        copy.start()
    greeters = has_right.astype(jnp.int32) + (has_left & ~lazy_left).astype(jnp.int32)
    ushered = (head != 0) & (head != USHER)
    pl.semaphore_wait(barrier, greeters + len(peers) - ushered.astype(jnp.int32))

    def remote(src, dst, send, recv, **who):
        return pltpu.make_async_remote_copy(
            src_ref=src, dst_ref=dst, send_sem=send, recv_sem=recv,
            device_id=who, device_id_type=MESH,
        )

    kv1, kv2, delta_copies = {}, {}, {}
    for c in range(NC):
        kv1[c] = (
            remote(k_h.at[sl(c)], k1.at[sl(c)], s1.at[0, c], r1.at[0, c], rows=right),
            remote(v_h.at[sl(c)], v1.at[sl(c)], s1.at[1, c], r1.at[1, c], rows=right),
        )
        kv2[c] = (
            remote(k1.at[sl(c)], k2.at[sl(c)], s2.at[0, c], r2.at[0, c], rows=right),
            remote(v1.at[sl(c)], v2.at[sl(c)], s2.at[1, c], r2.at[1, c], rows=right),
        )
        delta_copies[c] = (
            remote(d0.at[sl(c)], d1.at[sl(c)], sd.at[0, c], rd.at[0, c], rows=left),
            remote(d1.at[sl(c)], d2.at[sl(c)], sd.at[1, c], rd.at[1, c], rows=left),
        )
    o_copies = [
        remote(o_out.at[sl(c)], o_in.at[sl(c)], so.at[c], ro.at[c], rows=right)
        for c in range(NC)
    ]
    q_copies = (
        remote(q_h, q1, sq.at[0], rq.at[0], rows=left),
        remote(q1, q2, sq.at[1], rq.at[1], rows=left),
    )

    @pl.when(has_right)
    def _():
        for c in reversed(range(NC)):
            for copy in kv1[c]:
                copy.start()

    @pl.when(lazy_right)
    def _():
        pl.semaphore_signal(left_sem, inc=1, device_id={"rows": right}, device_id_type=MESH)

    @pl.when(head == USHER)
    def _():
        for who in peers:
            @pl.when(who != 0)
            def _():
                pl.semaphore_signal(usher_sem, inc=1, device_id={"heads": who}, device_id_type=MESH)

    @pl.when(lazy_left)
    def _():
        pl.semaphore_wait(left_sem, 1)

    @pl.when(has_left)
    def _():
        q_copies[0].start()

    for copy in loads:
        copy.wait()

    first_row = pos * R
    for c in range(NC):
        for row, dst in ((0, srel), (1, erel)):
            line = bnd[row : row + 1, c * CH : (c + 1) * CH] - first_row
            dst[sl(c), :] = jnp.transpose(jnp.broadcast_to(line, (CH, CH)))

    def parts(raw, allowed):
        raw = jnp.where(allowed, raw, MASKED)
        scores = raw * factor
        sigmoid = 1.0 / (1.0 + jnp.exp2(raw * (-factor * LOG2E)))
        weights = scores * sigmoid
        return weights, sigmoid * ((1.0 + scores) - weights)

    def lanes(n, base):
        return lax.broadcasted_iota(jnp.int32, (n * CH, CH), 1) + base

    def sublanes(n, base):
        return lax.broadcasted_iota(jnp.int32, (n * CH, CH), 0) + base

    def halves(value, w):
        return [value[:, m * CH : (m + 1) * CH] for m in range(w)]

    def joined(values):
        return values[0] if len(values) == 1 else jnp.concatenate(values, axis=1)

    def forward(c, w, off, kk, vv, lo, hi, fresh=False):
        n = hi - lo
        packed = []
        for m, raw in enumerate(halves(dot_nt(qb[sl(lo, n), :], kk[sl(c, w), :]), w)):
            at = lanes(n, (c + m) * CH - off * R)
            allowed = at >= srel[sl(lo, n), :]
            if off == 0:
                allowed = allowed & (at <= sublanes(n, lo * CH))
            weights, slope = parts(raw, allowed)
            fq[off, c + m, sl(lo, n), :] = slope
            packed.append(weights.astype(BF16))
        term = dot_nn(joined(packed), vv[sl(c, w), :])
        if fresh:
            att[sl(lo, n), :] = term
        else:
            att[sl(lo, n), :] += term

    def bridge(c, w, hi):
        first, last = srel[R - 1 : R, :], erel[R - 1 : R, :]
        packed = []
        for m, raw in enumerate(halves(dot_nt(q1[sl(0, hi), :], k1[sl(c, w), :]), w)):
            allowed = (lanes(hi, (c + m) * CH - R) >= first) & (sublanes(hi, R) <= last)
            packed.append(parts(raw, allowed)[0].astype(BF16))
        term = dot_nn(joined(packed), v1[sl(c, w), :])
        if hi == NC:
            far[...] = term
        else:
            far[sl(0, hi), :] += term
        for i in reversed(range(c, hi)):
            o_out[sl(i), :] = far[sl(i), :].astype(BF16)
            o_copies[i].start()

    def far_slopes(c, w, hi):
        for m, raw in enumerate(halves(dot_nt(qb[sl(0, hi), :], k2[sl(c, w), :]), w)):
            allowed = lanes(hi, (c + m) * CH - 2 * R) >= srel[sl(0, hi), :]
            fq[2, c + m, sl(0, hi), :] = parts(raw, allowed)[1]

    def prepare(i, w, off, qq, lo, hi):
        n = hi - lo
        for m, raw in enumerate(halves(dot_nt(kb[sl(lo, n), :], qq[sl(i, w), :]), w)):
            at = lanes(n, (i + m) * CH + off * R)
            allowed = at <= erel[sl(lo, n), :]
            if off == 0:
                allowed = allowed & (at >= sublanes(n, lo * CH))
            weights, slope = parts(raw, allowed)
            ft[off, i + m, sl(lo, n), :] = slope
            pt[off, i + m, sl(lo, n), :] = weights.astype(BF16)

    def stats_copies(c):
        return [
            remote(
                st_out.at[c], st_in.at[head, c], ss.at[p, c], rs.at[head, c], heads=who
            )
            for p, who in enumerate(peers)
        ]

    def stats_send(i):
        rows_t = jnp.transpose(att[sl(i), :])
        scaled_t = jnp.transpose(cb[sl(i), :].astype(F32) * gb[sl(i), :].astype(F32))
        for n, term in enumerate((rows_t, rows_t * rows_t, scaled_t, scaled_t * rows_t)):
            st_out[i, n : n + 1, :] = jnp.sum(term, axis=0, keepdims=True)
        st_in[head, i, 0:4, :] = st_out[i, 0:4, :]
        for copy in stats_copies(i):
            copy.start()

    def stats_use(i):
        for who in peers:
            remote(
                st_out.at[i], st_in.at[who, i], ss.at[0, i], rs.at[who, i], heads=who
            ).wait_recv()
        total = st_in[0, i, 0:4, :]
        for p in range(1, heads_n):
            total = total + st_in[p, i, 0:4, :]
        average = total[0:1] / features
        inverse = lax.rsqrt(total[1:2] / features - average * average + EPSILON)
        grad_mean = total[2:3] / features
        cross_mean = inverse * (total[3:4] - average * total[2:3]) / features

        def column(line):
            return jnp.transpose(jnp.broadcast_to(line, (CH, CH)))

        inverse_c = column(inverse)
        normed = (att[sl(i), :] - column(average)) * inverse_c
        gate = gb[sl(i), :].astype(F32)
        upstream = cb[sl(i), :].astype(F32)
        delta = inverse_c * (
            upstream * gate - column(grad_mean) - normed * column(cross_mean)
        )
        d0[sl(i), :] = delta.astype(BF16)
        lay_o[sl(i), :] = (normed * gate).astype(BF16)
        gg_o[sl(i), :] = (upstream * normed).astype(BF16)

        @pl.when(has_left)
        def _():
            delta_copies[i][0].start()

    def query_grad(c, off, kk, vv, lo, hi, fresh=False):
        n = hi - lo
        pulled = dot_nt(d0[sl(lo, n), :], vv[sl(c, 2), :])
        slope = joined([fq[off, c + m, sl(lo, n), :] for m in range(2)])
        term = dot_nn((pulled * slope).astype(BF16), kk[sl(c, 2), :])
        if fresh:
            att[sl(lo, n), :] = term
        else:
            att[sl(lo, n), :] += term

    def query_own():
        query_grad(0, 0, kb, vb, 0, NC, fresh=True)
        query_grad(2, 0, kb, vb, 2, NC)

    def query_far():
        @pl.when(has_left)
        def _():
            query_grad(0, 1, k1, v1, 0, NC)
            query_grad(2, 1, k1, v1, 0, NC)

        @pl.when(has_left2)
        def _():
            query_grad(0, 2, k2, v2, 0, 2)
            query_grad(2, 2, k2, v2, 0, NC)

        gq_o[...] = (att[...] * factor).astype(BF16)

    def key_grad(i, off, qq, dd, lo, hi, fresh=False):
        n = hi - lo
        delta = dd[sl(i, 2), :]
        pulled = dot_nt(vb[sl(lo, n), :], delta)
        slope = joined([ft[off, i + m, sl(lo, n), :] for m in range(2)])
        key_add = dot_nn((pulled * slope).astype(BF16), qq[sl(i, 2), :])
        weights = joined([pt[off, i + m, sl(lo, n), :] for m in range(2)])
        value_add = dot_nn(weights, delta)
        if fresh:
            dk[sl(lo, n), :] = key_add
            dv[sl(lo, n), :] = value_add
        else:
            dk[sl(lo, n), :] += key_add
            dv[sl(lo, n), :] += value_add

    def relay(i):
        @pl.when(has_right)
        def _():
            delta_copies[i][0].wait_recv()

            @pl.when(has_left)
            def _():
                delta_copies[i][1].start()

    def near_grad(i):
        @pl.when(has_right)
        def _():
            key_grad(i, 1, q1, d1, 0, NC)

    def far_grad(i):
        @pl.when(has_right2)
        def _():
            for c in (i, i + 1):
                delta_copies[c][1].wait_recv()
            key_grad(i, 2, q2, d2, i, NC)

    def arrive(c):
        @pl.when(has_left2)
        def _():
            o_copies[c].wait_recv()
            att[sl(c), :] += o_in[sl(c), :].astype(F32)

        stats_send(c)

    def far_arrive():
        @pl.when(has_left2)
        def _():
            for c in reversed(range(NC)):
                for copy in kv2[c]:
                    copy.wait_recv()
            far_slopes(2, 2, NC)
            far_slopes(0, 2, 2)

    forward(0, 2, 0, kb, vb, 0, NC, fresh=True)
    forward(2, 2, 0, kb, vb, 2, NC)
    prepare(0, 2, 0, qb, 0, 2)
    prepare(2, 2, 0, qb, 0, NC)

    @pl.when(has_left)
    def _():
        for m in (3, 2):
            for copy in kv1[m]:
                copy.wait_recv()
        forward(2, 2, 1, k1, v1, 0, NC)

    @pl.when(has_right)
    def _():
        q_copies[0].wait_recv()

        @pl.when(has_left)
        def _():
            q_copies[1].start()
            bridge(2, 2, NC)

    for c in (1, 0):
        @pl.when(has_left)
        def _():
            for copy in kv1[c]:
                copy.wait_recv()

            @pl.when(has_right)
            def _():
                bridge(c, 1, c + 1)

            forward(c, 1, 1, k1, v1, 0, NC)

    @pl.when(has_left & has_right)
    def _():
        for c in reversed(range(NC)):
            for copy in kv2[c]:
                copy.start()

    @pl.when(ushered)
    def _():
        pl.semaphore_wait(usher_sem, 1)

    for c in reversed(range(NC)):
        arrive(c)

    @pl.when(has_right)
    def _():
        prepare(0, 2, 1, q1, 0, NC)
        prepare(2, 2, 1, q1, 0, NC)

    for c in reversed(range(NC)):
        stats_use(c)
    key_grad(2, 0, qb, d0, 0, NC, fresh=True)

    @pl.when(has_right2)
    def _():
        q_copies[1].wait_recv()
        prepare(0, 2, 2, q2, 0, NC)
        prepare(2, 2, 2, q2, 2, NC)

    relay(3)
    query_own()
    relay(2)
    key_grad(0, 0, qb, d0, 0, 2)
    relay(1)
    near_grad(2)
    relay(0)
    near_grad(0)
    far_arrive()
    query_far()
    far_grad(2)
    far_grad(0)
    gk_o[...] = (dk[...] * factor).astype(BF16)
    gv_o[...] = dv[...].astype(BF16)

    @pl.when(has_right)
    def _():
        for c in range(NC):
            for copy in kv1[c]:
                copy.wait_send()

    @pl.when(has_left & has_right)
    def _():
        for c in range(NC):
            o_copies[c].wait_send()
            for copy in kv2[c]:
                copy.wait_send()

    @pl.when(has_left)
    def _():
        q_copies[0].wait_send()
        for c in range(NC):
            delta_copies[c][0].wait_send()

    @pl.when(has_left & has_right)
    def _():
        q_copies[1].wait_send()
        for c in range(NC):
            delta_copies[c][1].wait_send()

    for c in range(NC):
        for copy in stats_copies(c):
            copy.wait_send()


def store_kernel(*refs):
    sources, results, sems = refs[:5], refs[5:10], refs[10]
    copies = [
        pltpu.make_async_copy(src, dst, sems.at[n])
        for n, (src, dst) in enumerate(zip(sources, results))
    ]
    for copy in copies:
        copy.start()
    for copy in copies:
        copy.wait()


def local(rows_n, heads_n, queries, key_vectors, value_vectors, gating, bounds, cotangent):
    R, width = queries.shape
    NC = R // CH
    block = (R, width)
    bf = lambda *shape: pltpu.VMEM(shape, BF16)
    fl = lambda *shape: pltpu.VMEM(shape, F32)
    dma = lambda *shape: pltpu.SemaphoreType.DMA(shape)
    out = jax.ShapeDtypeStruct(block, BF16)
    held = pl.pallas_call(
        functools.partial(kernel, rows_n, heads_n, DH ** (-0.5)),
        out_shape=(pltpu.VMEM(block, BF16),) * 5,
        in_specs=[pl.BlockSpec(memory_space=pl.ANY)] * 6,
        out_specs=(pl.BlockSpec(memory_space=pltpu.VMEM),) * 5,
        scratch_shapes=[
            pltpu.VMEM((2, R), jnp.int32),
            *[bf(*block)] * 5,
            *[bf(*block)] * 9,
            fl(*block), bf(*block), bf(*block),
            pltpu.VMEM((R, CH), jnp.int32), pltpu.VMEM((R, CH), jnp.int32),
            fl(3, NC, R, CH), fl(3, NC, R, CH), bf(3, NC, R, CH),
            fl(*block), fl(*block), fl(*block),
            fl(NC, 8, CH), fl(heads_n, NC, 8, CH),
            dma(6), dma(2, NC), dma(2, NC), dma(2, NC), dma(2, NC), dma(NC), dma(NC),
            dma(2), dma(2), dma(2, NC), dma(2, NC),
            dma(heads_n - 1, NC), dma(heads_n, NC), pltpu.SemaphoreType.REGULAR, pltpu.SemaphoreType.REGULAR,
        ],
        compiler_params=pltpu.CompilerParams(collective_id=0, has_side_effects=True),
        name="jagged_attention",
    )(bounds, queries, key_vectors, value_vectors, gating, cotangent)
    return pl.pallas_call(
        store_kernel,
        out_shape=(out,) * 5,
        in_specs=[pl.BlockSpec(memory_space=pltpu.VMEM)] * 5,
        out_specs=(pl.BlockSpec(memory_space=pl.ANY),) * 5,
        scratch_shapes=[dma(5)],
        name="store_outputs",
    )(*[pltpu.with_memory_space_constraint(x, pltpu.VMEM) for x in held])


def solution(mesh):
    spec = P("rows", "heads")
    return jax.shard_map(
        functools.partial(local, mesh.shape["rows"], mesh.shape["heads"]),
        mesh=mesh,
        in_specs=(spec, spec, spec, spec, P(None, "rows"), spec),
        out_specs=(spec,) * 5,
        check_vma=False,
    )
```
